512 devices in a mesh: sec: 64 (over y, z), mpo: 8 (over x, core).
Axes of the slice: x: 4, y: 4, z: 16, core: 2. Of those that a mesh axis runs over, the one named last changes fastest.
Arguments:
- wavefunction: bfloat16 [64, 8, 512, 256], P('sec', None, 'mpo'), may hold values from -6 to 6
- left_env: bfloat16 [64, 40, 512, 512], P('sec', 'mpo'), may hold values from -0.0390625 to 0.0390625
- right_env: bfloat16 [64, 40, 256, 256], P('sec', 'mpo'), may hold values from -0.375 to 0.375
- left_dims: int32 [64], P('sec'), may hold values from 256 to 512
- right_dims: int32 [64], P('sec'), may hold values from 128 to 256
- term_shift: int32 [40], P('mpo'), may hold values from 0 to 4, as said below
Outputs:
- product: bfloat16 [64, 8, 512, 256], P('sec', None, 'mpo')
The draws below stay inside these ranges and needn't reach their ends.
Inputs may be any that keep to these rules, and one draw needn't show every extreme that they name: `term_shift`: each of the five classes is named by exactly 8 terms.
All inputs are finite; a program needn't handle non-finite values.
Results may differ from the reference program's by a relative error of at most 0.0049.
Values may be sent and summed in bfloat16 or wider, within the bound.
A program may use at most 64 MiB of HBM per device.

```python
import jax
import jax.numpy as jnp
from jax import lax

P_SIZE = 512
Q = 256
TERMS = 40
SPINS = 8
NVEC = 8
SECTORS = 64


def draw_left_dims(key, part):
    drawn = jax.random.randint(key, (SECTORS,), P_SIZE // 2, P_SIZE + 1).astype(jnp.int32)
    return drawn.at[0].set(P_SIZE).at[1].set(P_SIZE // 2)


def draw_right_dims(key, part):
    drawn = jax.random.randint(key, (SECTORS,), Q // 2, Q + 1).astype(jnp.int32)
    return drawn.at[1].set(Q).at[0].set(Q // 2)


def draw_term_shift(key, part):
    return (jax.random.permutation(key, TERMS) % 5).astype(jnp.int32)


def steps_of(rng, extent, pieces, least, largest):
    gain, own = 1.0, jax.random.fold_in(rng, 6)
    for position, shards_of in pieces:
        steps = jnp.exp(jax.random.uniform(jax.random.fold_in(own, position), (shards_of,), jnp.float32, least / len(pieces), largest / len(pieces)))
        gain = gain * jnp.repeat(steps, extent[position] // shards_of).reshape([-1 if axis == position else 1 for axis in range(len(extent))])
    return gain


def centred(key, extent, deviation, reach, cuts=(), kind=jnp.bfloat16):
    array = deviation * jax.random.normal(key, extent, jnp.float32)
    if cuts:
        array = array * steps_of(key, extent, cuts, -0.22, 0.18)
    return jnp.clip(array, -reach, reach).astype(kind)


def setup_inputs(seed: int = 0) -> dict:
    keys = jax.random.split(jax.random.key(seed), 7)
    return {
        "wavefunction": centred(keys[0], (SECTORS, NVEC, P_SIZE, Q), 1.0, 6.0, ((0, 64), (2, 8))),
        "left_env": centred(keys[1], (SECTORS, TERMS, P_SIZE, P_SIZE), (P_SIZE * TERMS) ** -0.5, 0.0390625, ((0, 64), (1, 8))),
        "right_env": centred(keys[2], (SECTORS, TERMS, Q, Q), Q ** -0.5, 0.375, ((0, 64), (1, 8))),
        "left_dims": draw_left_dims(jax.random.fold_in(keys[6], 71), 0),
        "right_dims": draw_right_dims(jax.random.fold_in(keys[6], 71), 0),
        "term_shift": draw_term_shift(jax.random.fold_in(keys[6], 71), 0),
    }


number_steps = (0, 1, -1, 1, -1)
spin_steps = (0, 1, -1, -1, 1)


def reference(wavefunction, left_env, right_env, left_dims, right_dims, term_shift):
    row_ids = jnp.arange(P_SIZE, dtype=jnp.int32)
    column_ids = jnp.arange(Q, dtype=jnp.int32)
    row_mask = row_ids[None, :] < left_dims[:, None]
    column_mask = column_ids[None, :] < right_dims[:, None]
    keep_mask = row_mask[:, None, :, None] & column_mask[:, None, None, :]
    live_block = jnp.where(keep_mask, wavefunction, jnp.zeros_like(wavefunction))
    selector = (term_shift[:, None] == jnp.arange(5, dtype=jnp.int32)[None, :]).astype(jnp.float32)
    lattice_rows = SECTORS // SPINS

    def one_sector(sector_id):
        sector_line = sector_id // SPINS
        sector_place = sector_id % SPINS
        sources = []
        for shift_class in range(5):
            source_line = sector_line - number_steps[shift_class]
            source_place = sector_place - spin_steps[shift_class]
            inside = (source_line >= 0) & (source_line < lattice_rows) & (source_place >= 0) & (source_place < SPINS)
            source_id = jnp.clip(source_line * SPINS + source_place, 0, SECTORS - 1).astype(jnp.int32)
            neighbour = lax.dynamic_index_in_dim(live_block, source_id, 0, keepdims=False).astype(jnp.float32)
            sources.append(neighbour * inside.astype(jnp.float32))
        stacked = jnp.stack(sources)
        selected = jnp.einsum('tc,cvpq->tvpq', selector, stacked)
        left_block = lax.dynamic_index_in_dim(left_env, sector_id, 0, keepdims=False).astype(jnp.float32)
        right_block = lax.dynamic_index_in_dim(right_env, sector_id, 0, keepdims=False).astype(jnp.float32)
        applied = jnp.einsum('tpk,tvkq->tvpq', left_block, selected).astype(jnp.bfloat16)
        applied = lax.optimization_barrier(applied).astype(jnp.float32)
        return jnp.einsum('tvpk,tqk->vpq', applied, right_block)

    total = lax.map(one_sector, jnp.arange(SECTORS, dtype=jnp.int32))
    return jnp.where(keep_mask, total, jnp.zeros_like(total)).astype(jnp.bfloat16)
```

```python
import functools

import jax
import jax.numpy as jnp
from jax import lax
from jax.experimental import pallas as pl
from jax.experimental.pallas import tpu as pltpu
from jax.sharding import PartitionSpec as P

SPINS = 8
MESH = pl.DeviceIdType.MESH
CHUNKS = 4
OWN, LOW, HIGH, FAR_LOW, FAR_HIGH, NOTHING = range(6)


def kernel(
    shift_ref, left_dim, right_dim, shift_any, wave, left, right, out,
    src0, src1, src2, src3, lbuf, rbuf, acc, rs_out, rs_in, shift2, slots,
    local_sem, pair_send, pair_recv, env_local, env_send, env_recv,
    z_send, z_recv, y_send, y_recv, x_send, xl, xr, rl, rr, rs_send, rs_recv,
):
    sources = (src0, src1, src2, src3)
    share, columns = wave.shape[1], wave.shape[2]
    terms = left.shape[0]
    m = lax.axis_index("mpo")
    s = lax.axis_index("sec")
    x, core = lax.div(m, 2), lax.rem(m, 2)
    y, z = lax.div(s, 16), lax.rem(s, 16)
    half, place = lax.div(z, 8), lax.rem(z, 8)
    other = 1 - core
    partner = 2 * x + other
    to_right, to_left = lax.rem(m + 2, 8), lax.rem(m + 6, 8)
    x_low, x_high = lax.rem(x + 3, 4), lax.rem(x + 1, 4)
    z_up = y * 16 + lax.rem(z + 7, 16)
    z_down = y * 16 + lax.rem(z + 9, 16)
    y_plus = lax.rem(y + 1, 4) * 16 + z
    y_minus = lax.rem(y + 3, 4) * 16 + z
    y_next = lax.rem(y + 1 + 2 * half, 4) * 16 + z

    def rows(start, count):
        return pl.ds(pl.multiple_of(start, share), count)

    mine = rows(m * share, share)
    block = rows(x * 2 * share, 2 * share)

    def send(src, dst, ssem, rsem, sec, mpo):
        pltpu.make_async_remote_copy(
            src_ref=src, dst_ref=dst, send_sem=ssem, recv_sem=rsem,
            device_id={"sec": sec, "mpo": mpo}, device_id_type=MESH,
        ).start()

    def await_bytes(ref, sem):
        pltpu.make_async_copy(ref, ref, sem).wait()

    own_vectors = pl.multiple_of(core * CHUNKS, CHUNKS)
    local = []
    for i in range(CHUNKS):
        local.append(
            pltpu.make_async_copy(
                wave.at[core * CHUNKS + i], sources[i].at[OWN, mine], local_sem.at[i]
            )
        )
    local.append(pltpu.make_async_copy(left, lbuf.at[pl.ds(0, terms)], env_local.at[0]))
    local.append(pltpu.make_async_copy(right, rbuf.at[pl.ds(0, terms)], env_local.at[1]))

    barrier = pltpu.get_barrier_semaphore()
    for core_id in range(2):
        for sec in (z_up, z_down):
            pl.semaphore_signal(
                barrier, inc=1, device_id={"sec": sec, "mpo": 2 * x + core_id},
                device_id_type=MESH,
            )
    for sec in (y_plus, y_minus):
        pl.semaphore_signal(
            barrier, inc=1, device_id={"sec": sec, "mpo": m}, device_id_type=MESH
        )
    for k in range(1, 8):
        pl.semaphore_signal(
            barrier, inc=1, device_id={"sec": s, "mpo": lax.rem(m + k, 8)},
            device_id_type=MESH,
        )
    for copy in local:
        copy.start()
    for i in range(CHUNKS):
        sources[i][NOTHING] = jnp.zeros(sources[i].shape[1:], sources[i].dtype)
    pl.semaphore_wait(barrier, 13)

    for i in range(CHUNKS):
        send(
            wave.at[other * CHUNKS + i], sources[i].at[OWN, mine],
            pair_send.at[i], pair_recv.at[i], s, partner,
        )
    for i in range(CHUNKS):
        for core_id in range(2):
            for slot, sec in ((LOW, z_up), (HIGH, z_down)):
                send(
                    wave.at[core_id * CHUNKS + i], sources[i].at[slot, mine],
                    z_send.at[i], z_recv.at[slot - LOW, i], sec, 2 * x + core_id,
                )
    send(shift_any, shift2, env_send.at[2], env_recv.at[2], s, partner)
    send(left, lbuf.at[pl.ds(terms, terms)], env_send.at[0], env_recv.at[0], s, partner)
    send(right, rbuf.at[pl.ds(terms, terms)], env_send.at[1], env_recv.at[1], s, partner)

    def x_start(slot, i):
        part = sources[i].at[slot, block]
        send(part, part, x_send.at[slot, i], xl.at[slot, i], s, to_right)
        send(part, part, x_send.at[slot, i], xr.at[slot, i], s, to_left)

    def x_relay(slot, i):
        low = rows(x_low * 2 * share, 2 * share)
        low_first = rows(x_low * 2 * share, share)
        await_bytes(sources[i].at[slot, low], xl.at[slot, i])
        part = sources[i].at[slot, low_first]
        send(part, part, x_send.at[slot, i], rl.at[slot, i], s, to_right)
        high = rows(x_high * 2 * share, 2 * share)
        high_last = rows(x_high * 2 * share + share, share)
        await_bytes(sources[i].at[slot, high], xr.at[slot, i])
        part = sources[i].at[slot, high_last]
        send(part, part, x_send.at[slot, i], rr.at[slot, i], s, to_left)

    def x_finish(slot, i):
        await_bytes(sources[i].at[slot, pl.ds(0, share)], rl.at[slot, i])
        await_bytes(sources[i].at[slot, pl.ds(0, share)], rr.at[slot, i])

    def product(i, first, last):
        @pl.loop(first, last)
        def _(t):
            applied = jnp.dot(
                lbuf[t], sources[i][slots[t]], preferred_element_type=jnp.float32
            ).astype(jnp.bfloat16)
            part = lax.dot_general(
                applied, rbuf[t], (((1,), (1,)), ((), ())),
                preferred_element_type=jnp.float32,
            )
            acc[...] += part

    def sums_start(i):
        for k in range(8):
            rs_out[i, k] = acc[pl.ds(k * share, share), :].astype(jnp.bfloat16)
        rs_in[x, core * CHUNKS + i] = acc[mine, :].astype(jnp.bfloat16)
        for k in range(1, 8):
            target = lax.rem(m + k, 8)
            send(
                rs_out.at[i, target], rs_in.at[x, core * CHUNKS + i],
                rs_send.at[i], rs_recv.at[i], s, target,
            )
        acc[...] = jnp.zeros_like(acc)

    row_ids = m * share + lax.broadcasted_iota(jnp.int32, (share, columns), 0)
    column_ids = lax.broadcasted_iota(jnp.int32, (share, columns), 1)
    keep = (row_ids < left_dim[0]) & (column_ids < right_dim[0])

    def sums_finish(i):
        await_bytes(rs_out.at[i, pl.ds(0, 7)], rs_recv.at[i])
        for v in (i, CHUNKS + i):
            total = rs_in[0, v].astype(jnp.float32)
            for k in range(1, 4):
                total = total + rs_in[k, v].astype(jnp.float32)
            out[v] = jnp.where(keep, total, jnp.zeros_like(total)).astype(out.dtype)

    for i in range(CHUNKS):
        local[i].wait()
        await_bytes(sources[i].at[OWN, mine], pair_recv.at[i])
        x_start(OWN, i)
    for i in range(CHUNKS):
        x_relay(OWN, i)
    acc[...] = jnp.zeros_like(acc)

    low_ok = place <= 6
    high_ok = place >= 1
    far_ok = jnp.where(half == 1, y <= 2, y >= 1)
    low_slot = jnp.where(low_ok, LOW, NOTHING)
    high_slot = jnp.where(high_ok, HIGH, NOTHING)
    far_low_slot = jnp.where(low_ok & far_ok, FAR_LOW, NOTHING)
    far_high_slot = jnp.where(high_ok & far_ok, FAR_HIGH, NOTHING)
    class_slots = (
        OWN,
        jnp.where(half == 1, high_slot, far_high_slot),
        jnp.where(half == 1, far_low_slot, low_slot),
        jnp.where(half == 1, low_slot, far_low_slot),
        jnp.where(half == 1, far_high_slot, high_slot),
    )

    def slot_of(shift):
        found = jnp.int32(OWN)
        for c in range(1, 5):
            found = jnp.where(shift == c, class_slots[c], found)
        return found

    await_bytes(shift2, env_recv.at[2])
    for t in range(terms):
        slots[t] = slot_of(shift_ref[t])
        slots[terms + t] = slot_of(shift2[t])

    for i in range(CHUNKS):
        for slot in (LOW, HIGH):
            await_bytes(sources[i].at[slot, block], z_recv.at[slot - LOW, i])
            part = sources[i].at[slot, block]
            send(
                part, sources[i].at[slot + 2, block],
                y_send.at[i], y_recv.at[slot - LOW, i], y_next, m,
            )
            x_start(slot, i)
        if i == 1:
            local[CHUNKS].wait()
            local[CHUNKS + 1].wait()
            await_bytes(lbuf.at[pl.ds(terms, terms)], env_recv.at[0])
            await_bytes(rbuf.at[pl.ds(terms, terms)], env_recv.at[1])
        if i > 0:
            product(i - 1, 0, terms)
        for slot in (LOW, HIGH):
            x_relay(slot, i)
        for slot in (FAR_LOW, FAR_HIGH):
            await_bytes(sources[i].at[slot, block], y_recv.at[slot - FAR_LOW, i])
            x_start(slot, i)
        if i > 0:
            product(i - 1, terms, 2 * terms)
            sums_start(i - 1)
        for slot in (FAR_LOW, FAR_HIGH):
            x_relay(slot, i)
        for slot in range(5):
            x_finish(slot, i)
        if i > 1:
            sums_finish(i - 2)
    product(CHUNKS - 1, 0, 2 * terms)
    sums_start(CHUNKS - 1)
    sums_finish(CHUNKS - 2)
    sums_finish(CHUNKS - 1)

    for i in range(CHUNKS):
        await_bytes(sources[i].at[OWN, pl.ds(0, share)], pair_send.at[i])
        await_bytes(sources[i].at[OWN, pl.ds(0, 4 * share)], z_send.at[i])
        await_bytes(sources[i].at[OWN, pl.ds(0, 4 * share)], y_send.at[i])
        await_bytes(rs_out.at[i, pl.ds(0, 7)], rs_send.at[i])
        for slot in range(5):
            await_bytes(sources[i].at[slot, pl.ds(0, 6 * share)], x_send.at[slot, i])
    await_bytes(lbuf.at[pl.ds(0, terms)], env_send.at[0])
    await_bytes(rbuf.at[pl.ds(0, terms)], env_send.at[1])
    await_bytes(shift2, env_send.at[2])


def per_device(wavefunction, left_env, right_env, left_dims, right_dims, term_shift):
    _, vectors, share, columns = wavefunction.shape
    full = left_env.shape[2]
    terms = left_env.shape[1]
    rows_here = lax.axis_index("mpo") * share + jnp.arange(share, dtype=jnp.int32)
    column_ids = jnp.arange(columns, dtype=jnp.int32)
    keep = (rows_here[:, None] < left_dims[0]) & (column_ids[None, :] < right_dims[0])
    live = jnp.where(keep[None], wavefunction[0], jnp.zeros_like(wavefunction[0]))
    smem = pl.BlockSpec(memory_space=pltpu.SMEM)
    anywhere = pl.BlockSpec(memory_space=pl.ANY)
    bf16 = jnp.bfloat16
    dma = pltpu.SemaphoreType.DMA
    out = pl.pallas_call(
        kernel,
        out_shape=jax.ShapeDtypeStruct((vectors, share, columns), bf16),
        in_specs=[smem, smem, smem, anywhere, anywhere, anywhere, anywhere],
        out_specs=pl.BlockSpec(memory_space=pltpu.VMEM),
        scratch_shapes=[pltpu.VMEM((6, full, columns), bf16) for _ in range(CHUNKS)]
        + [
            pltpu.VMEM((2 * terms, full, full), bf16),
            pltpu.VMEM((2 * terms, columns, columns), bf16),
            pltpu.VMEM((full, columns), jnp.float32),
            pltpu.VMEM((CHUNKS, 8, share, columns), bf16),
            pltpu.VMEM((4, vectors, share, columns), bf16),
            pltpu.SMEM((terms,), jnp.int32),
            pltpu.SMEM((2 * terms,), jnp.int32),
            dma((CHUNKS,)), dma((CHUNKS,)), dma((CHUNKS,)),
            dma((2,)), dma((3,)), dma((3,)),
            dma((CHUNKS,)), dma((2, CHUNKS)), dma((CHUNKS,)), dma((2, CHUNKS)),
            dma((5, CHUNKS)), dma((5, CHUNKS)), dma((5, CHUNKS)),
            dma((5, CHUNKS)), dma((5, CHUNKS)),
            dma((CHUNKS,)), dma((CHUNKS,)),
        ],
        compiler_params=pltpu.CompilerParams(
            collective_id=0, has_side_effects=True, vmem_limit_bytes=60 * 1024 * 1024
        ),
    )(term_shift, left_dims, right_dims, term_shift, live, left_env[0], right_env[0])
    return out[None]


def solution(mesh):
    in_specs = (
        P("sec", None, "mpo", None),
        P("sec", "mpo", None, None),
        P("sec", "mpo", None, None),
        P("sec"),
        P("sec"),
        P("mpo"),
    )
    out_specs = P("sec", None, "mpo", None)
    return jax.shard_map(
        per_device, mesh=mesh, in_specs=in_specs, out_specs=out_specs, check_vma=False
    )
```

```python
import jax
import jax.numpy as jnp
from jax import lax
from jax.experimental import pallas as pl
from jax.experimental.pallas import tpu as pltpu
from jax.sharding import PartitionSpec as P

SPINS = 8
MESH = pl.DeviceIdType.MESH
CHUNKS = 4
OWN, LOW, HIGH, FAR_LOW, FAR_HIGH, NOTHING = range(6)
FROM_LOW, FROM_HIGH, REST = range(3)
GATHER_FIRST = frozenset((LOW, i) for i in range(CHUNKS))
PACE = 2
FIRST_NEAR = 9.5
CHUNK_TIME = 6.5
RELAYED = 4.0
ACROSS = 3.0
FIRST_OWN = 3.0
PIECES = 5


def kernel(
    shift_ref, left_dim, right_dim, shift_any, wave, left, right, out,
    src0, src1, src2, src3, lbuf, rbuf, acc, rs_out, rs_in, shift2, slots,
    local_sem, pair_send, pair_recv, env_local, env_send, env_recv,
    z_send, z_recv, y_send, y_recv, x_send, x_recv, rs_send, rs_recv,
):
    sources = (src0, src1, src2, src3)
    share, columns = wave.shape[1], wave.shape[2]
    terms = left.shape[0]
    m = lax.axis_index("mpo")
    s = lax.axis_index("sec")
    x, core = lax.div(m, 2), lax.rem(m, 2)
    y, z = lax.div(s, 16), lax.rem(s, 16)
    half, place = lax.div(z, 8), lax.rem(z, 8)
    other = 1 - core
    partner = 2 * x + other
    to_right, to_left = lax.rem(m + 2, 8), lax.rem(m + 6, 8)
    x_low, x_high, x_far = lax.rem(x + 3, 4), lax.rem(x + 1, 4), lax.rem(x + 2, 4)

    def along_z(step):
        return y * 16 + lax.rem(z + step + 16, 16)

    z_first = along_z(7 - 14 * core)
    y_plus = lax.rem(y + 1, 4) * 16 + z
    y_minus = lax.rem(y + 3, 4) * 16 + z
    y_next = lax.rem(y + 1 + 2 * half, 4) * 16 + z

    def rows(start, count):
        return pl.ds(pl.multiple_of(start, share), count)

    def piece(chip, side):
        return rows((2 * chip + side) * share, share)

    mine = rows(m * share, share)

    def send(src, dst, ssem, rsem, sec, mpo):
        pltpu.make_async_remote_copy(
            src_ref=src, dst_ref=dst, send_sem=ssem, recv_sem=rsem,
            device_id={"sec": sec, "mpo": mpo}, device_id_type=MESH,
        ).start()

    def await_bytes(ref, sem):
        pltpu.make_async_copy(ref, ref, sem).wait()

    local = []
    for i in range(CHUNKS):
        local.append(
            pltpu.make_async_copy(
                wave.at[core * CHUNKS + i], sources[i].at[OWN, mine], local_sem.at[i]
            )
        )
    local.append(pltpu.make_async_copy(left, lbuf.at[pl.ds(0, terms)], env_local.at[0]))
    local.append(pltpu.make_async_copy(right, rbuf.at[pl.ds(0, terms)], env_local.at[1]))

    barrier = pltpu.get_barrier_semaphore()

    def greet(sec, mpo):
        pl.semaphore_signal(
            barrier, inc=1, device_id={"sec": sec, "mpo": mpo}, device_id_type=MESH
        )

    for step in (7, -7):
        for core_id in range(2):
            greet(along_z(step), 2 * x + core_id)
    for sec in (along_z(2), along_z(-2), y_plus, y_minus):
        greet(sec, m)
    for k in range(1, 8):
        greet(s, lax.rem(m + k, 8))
    for copy in local:
        copy.start()
    for i in range(CHUNKS):
        sources[i][NOTHING] = jnp.zeros(sources[i].shape[1:], sources[i].dtype)
    acc[...] = jnp.zeros_like(acc)

    low_ok = place <= 6
    high_ok = place >= 1
    far_ok = jnp.where(half == 1, y <= 2, y >= 1)
    low_slot = jnp.where(low_ok, LOW, NOTHING)
    high_slot = jnp.where(high_ok, HIGH, NOTHING)
    far_low_slot = jnp.where(low_ok & far_ok, FAR_LOW, NOTHING)
    far_high_slot = jnp.where(high_ok & far_ok, FAR_HIGH, NOTHING)
    class_slots = (
        OWN,
        jnp.where(half == 1, high_slot, far_high_slot),
        jnp.where(half == 1, far_low_slot, low_slot),
        jnp.where(half == 1, low_slot, far_low_slot),
        jnp.where(half == 1, far_high_slot, high_slot),
    )

    def slot_of(shift):
        found = jnp.int32(OWN)
        for c in range(1, 5):
            found = jnp.where(shift == c, class_slots[c], found)
        return found

    row_ids = m * share + lax.broadcasted_iota(jnp.int32, (share, columns), 0)
    column_ids = lax.broadcasted_iota(jnp.int32, (share, columns), 1)
    keep = (row_ids < left_dim[0]) & (column_ids < right_dim[0])
    pl.semaphore_wait(barrier, 15)

    def z_start(i):
        @pl.when(core == 0)
        def _():
            for core_id in range(2):
                send(
                    wave.at[core_id * CHUNKS + i], sources[i].at[LOW, mine],
                    z_send.at[i], z_recv.at[0, 0, i], along_z(7), 2 * x + core_id,
                )

        @pl.when(core == 1)
        def _():
            for core_id in range(2):
                send(
                    wave.at[core_id * CHUNKS + i], sources[i].at[HIGH, mine],
                    z_send.at[i], z_recv.at[1, 1, i], along_z(-7), 2 * x + core_id,
                )

    for i in range(PACE):
        z_start(i)
    for i in range(CHUNKS):
        send(
            wave.at[other * CHUNKS + i], sources[i].at[OWN, mine],
            pair_send.at[i], pair_recv.at[i], s, partner,
        )
    send(shift_any, shift2, env_send.at[2], env_recv.at[2], s, partner)
    send(left, lbuf.at[pl.ds(terms, terms)], env_send.at[0], env_recv.at[0], s, partner)
    send(right, rbuf.at[pl.ds(terms, terms)], env_send.at[1], env_recv.at[1], s, partner)

    def x_part(slot, i, part, to, role):
        send(part, part, x_send.at[slot, i], x_recv.at[role, slot, i], s, to)

    def y_part(slot, i, which):
        send(
            sources[i].at[slot, which], sources[i].at[slot + 2, which],
            y_send.at[slot - LOW, i], y_recv.at[slot - LOW, 0, i], y_next, m,
        )

    def x_start(slot, i, side):
        part = sources[i].at[slot, piece(x, side)]
        x_part(slot, i, part, to_right, FROM_LOW if side == 0 else REST)
        x_part(slot, i, part, to_left, FROM_HIGH if side == 1 else REST)

    def x_relay(slot, i):
        for side, chip, to in ((0, x_low, to_right), (1, x_high, to_left)):
            part = sources[i].at[slot, piece(chip, side)]
            await_bytes(part, x_recv.at[side, slot, i])
            x_part(slot, i, part, to, REST)
            if (slot, i) in GATHER_FIRST:
                y_part(slot, i, piece(chip, side))

    def x_finish(slot, i):
        await_bytes(sources[i].at[slot, pl.ds(0, 4 * share)], x_recv.at[REST, slot, i])
        if (slot, i) in GATHER_FIRST:
            y_part(slot, i, piece(x_low, 1))
            y_part(slot, i, piece(x_high, 0))
            y_part(slot, i, rows(2 * x_far * share, 2 * share))

    def own_start(i):
        local[i].wait()
        await_bytes(sources[i].at[OWN, mine], pair_recv.at[i])
        x_start(OWN, i, 0)
        x_start(OWN, i, 1)

    def near_start(slot, side, i):
        await_bytes(sources[i].at[slot, piece(x, side)], z_recv.at[slot - LOW, side, i])
        which = piece(x, side)
        if slot - LOW == side:
            send(
                sources[i].at[slot, which], sources[i].at[LOW + HIGH - slot, which],
                z_send.at[i], z_recv.at[1 - side, side, i],
                along_z(2 - 4 * side), m,
            )
        if (slot, i) in GATHER_FIRST:
            y_part(slot, i, which)
        else:
            send(
                sources[i].at[slot, which], sources[i].at[slot + 2, which],
                y_send.at[slot - LOW, i], y_recv.at[slot - LOW, side, i], y_next, m,
            )
        x_start(slot, i, side)

    def far_start(slot, side, i):
        await_bytes(
            sources[i].at[slot + 2, piece(x, side)], y_recv.at[slot - LOW, side, i]
        )
        x_start(slot + 2, i, side)

    def far_finish(slot, i):
        await_bytes(sources[i].at[slot + 2], y_recv.at[slot - LOW, 0, i])

    def env_ready():
        await_bytes(shift2, env_recv.at[2])
        for t in range(terms):
            slots[t] = slot_of(shift_ref[t])
            slots[terms + t] = slot_of(shift2[t])
        local[CHUNKS].wait()
        local[CHUNKS + 1].wait()
        await_bytes(lbuf.at[pl.ds(terms, terms)], env_recv.at[0])
        await_bytes(rbuf.at[pl.ds(terms, terms)], env_recv.at[1])

    def product(i, first, last):
        for t in range(first, last):
            applied = jnp.dot(
                lbuf[t], sources[i][slots[t]], preferred_element_type=jnp.float32
            ).astype(jnp.bfloat16)
            acc[...] += lax.dot_general(
                applied, rbuf[t], (((1,), (1,)), ((), ())),
                preferred_element_type=jnp.float32,
            )

    def sums_start(i):
        for k in range(8):
            rs_out[i, k] = acc[pl.ds(k * share, share), :].astype(jnp.bfloat16)
        rs_in[x, core * CHUNKS + i] = acc[mine, :].astype(jnp.bfloat16)
        for k in range(1, 8):
            target = lax.rem(m + k, 8)
            send(
                rs_out.at[i, target], rs_in.at[x, core * CHUNKS + i],
                rs_send.at[i], rs_recv.at[i], s, target,
            )
        acc[...] = jnp.zeros_like(acc)

    def sums_finish(i):
        await_bytes(rs_out.at[i, pl.ds(0, 7)], rs_recv.at[i])
        for v in (i, CHUNKS + i):
            total = rs_in[0, v].astype(jnp.float32)
            for k in range(1, 4):
                total = total + rs_in[k, v].astype(jnp.float32)
            out[v] = jnp.where(keep, total, jnp.zeros_like(total)).astype(out.dtype)

    plan = []

    def at(when, function, *operands):
        plan.append((when, len(plan), function, operands))

    done = 0.0
    for i in range(CHUNKS):
        at(0.1 * i, own_start, i)
        at(FIRST_OWN + 2.1 * i, x_relay, OWN, i)
        base = FIRST_NEAR + CHUNK_TIME * i
        rel = base + RELAYED
        at(base, near_start, LOW, 0, i)
        at(base, near_start, HIGH, 1, i)
        if i + PACE < CHUNKS:
            at(base, z_start, i + PACE)
        at(rel, near_start, LOW, 1, i)
        at(rel, near_start, HIGH, 0, i)
        ready = rel + 8
        for slot in (LOW, HIGH):
            at(rel + 3, x_relay, slot, i)
            if (slot, i) in GATHER_FIRST:
                at(rel + 6, x_finish, slot, i)
                ready = max(ready, rel + 14)
            else:
                first = 0 if slot == LOW else 1
                at(base + ACROSS, far_start, slot, first, i)
                at(rel + ACROSS, far_start, slot, 1 - first, i)
                at(rel + ACROSS + 4, x_relay, slot + 2, i)
                ready = max(ready, rel + ACROSS + 8)
        done = max(done + 5.0, ready)
        at(done, x_finish, OWN, i)
        for slot in (LOW, HIGH):
            if (slot, i) in GATHER_FIRST:
                at(done, far_finish, slot, i)
            else:
                at(done, x_finish, slot, i)
                at(done, x_finish, slot + 2, i)
        if i == 0:
            at(done, env_ready)
        for k in range(PIECES):
            at(
                done + 5.0 * k / PIECES, product, i,
                2 * terms * k // PIECES, 2 * terms * (k + 1) // PIECES,
            )
        at(done + 4.9, sums_start, i)
        at(done + 100.0, sums_finish, i)
    for _, _, function, operands in sorted(plan, key=lambda entry: entry[:2]):
        function(*operands)

    for i in range(CHUNKS):
        await_bytes(sources[i].at[OWN, pl.ds(0, share)], pair_send.at[i])
        await_bytes(sources[i].at[OWN, pl.ds(0, 4 * share)], z_send.at[i])
        await_bytes(rs_out.at[i, pl.ds(0, 7)], rs_send.at[i])
        await_bytes(sources[i].at[OWN, pl.ds(0, 6 * share)], x_send.at[OWN, i])
        for slot in (LOW, HIGH):
            await_bytes(sources[i].at[slot, pl.ds(0, 6 * share)], x_send.at[slot, i])
            if (slot, i) in GATHER_FIRST:
                await_bytes(sources[i].at[slot], y_send.at[slot - LOW, i])
            else:
                await_bytes(
                    sources[i].at[slot, pl.ds(0, 2 * share)], y_send.at[slot - LOW, i]
                )
                await_bytes(
                    sources[i].at[slot, pl.ds(0, 6 * share)], x_send.at[slot + 2, i]
                )
    await_bytes(lbuf.at[pl.ds(0, terms)], env_send.at[0])
    await_bytes(rbuf.at[pl.ds(0, terms)], env_send.at[1])
    await_bytes(shift2, env_send.at[2])


def per_device(wavefunction, left_env, right_env, left_dims, right_dims, term_shift):
    _, vectors, share, columns = wavefunction.shape
    full = left_env.shape[2]
    terms = left_env.shape[1]
    rows_here = lax.axis_index("mpo") * share + jnp.arange(share, dtype=jnp.int32)
    column_ids = jnp.arange(columns, dtype=jnp.int32)
    keep = (rows_here[:, None] < left_dims[0]) & (column_ids[None, :] < right_dims[0])
    live = jnp.where(keep[None], wavefunction[0], jnp.zeros_like(wavefunction[0]))
    smem = pl.BlockSpec(memory_space=pltpu.SMEM)
    anywhere = pl.BlockSpec(memory_space=pl.ANY)
    bf16 = jnp.bfloat16
    dma = pltpu.SemaphoreType.DMA
    out = pl.pallas_call(
        kernel,
        out_shape=jax.ShapeDtypeStruct((vectors, share, columns), bf16),
        in_specs=[smem, smem, smem, anywhere, anywhere, anywhere, anywhere],
        out_specs=pl.BlockSpec(memory_space=pltpu.VMEM),
        scratch_shapes=[pltpu.VMEM((6, full, columns), bf16) for _ in range(CHUNKS)]
        + [
            pltpu.VMEM((2 * terms, full, full), bf16),
            pltpu.VMEM((2 * terms, columns, columns), bf16),
            pltpu.VMEM((full, columns), jnp.float32),
            pltpu.VMEM((CHUNKS, 8, share, columns), bf16),
            pltpu.VMEM((4, vectors, share, columns), bf16),
            pltpu.SMEM((terms,), jnp.int32),
            pltpu.SMEM((2 * terms,), jnp.int32),
            dma((CHUNKS,)), dma((CHUNKS,)), dma((CHUNKS,)),
            dma((2,)), dma((3,)), dma((3,)),
            dma((CHUNKS,)), dma((2, 2, CHUNKS)), dma((2, CHUNKS)), dma((2, 2, CHUNKS)),
            dma((5, CHUNKS)), dma((3, 5, CHUNKS)),
            dma((CHUNKS,)), dma((CHUNKS,)),
        ],
        compiler_params=pltpu.CompilerParams(
            collective_id=0, has_side_effects=True, vmem_limit_bytes=60 * 1024 * 1024
        ),
    )(term_shift, left_dims, right_dims, term_shift, live, left_env[0], right_env[0])
    return out[None]


def solution(mesh):
    in_specs = (
        P("sec", None, "mpo", None),
        P("sec", "mpo", None, None),
        P("sec", "mpo", None, None),
        P("sec"),
        P("sec"),
        P("mpo"),
    )
    out_specs = P("sec", None, "mpo", None)
    return jax.shard_map(
        per_device, mesh=mesh, in_specs=in_specs, out_specs=out_specs, check_vma=False
    )
```

```python
import jax
import jax.numpy as jnp
from jax import lax
from jax.experimental import pallas as pl
from jax.experimental.pallas import tpu as pltpu
from jax.sharding import PartitionSpec as P

SPINS = 8
MESH = pl.DeviceIdType.MESH
CHUNKS = 4
OWN, LOW, HIGH, FAR_LOW, FAR_HIGH, NOTHING = range(6)
FROM_LOW, FROM_HIGH, REST = range(3)
GATHER_FIRST = frozenset((LOW, i) for i in range(CHUNKS))
PACE = 2
FIRST_NEAR = 9.5
CHUNK_TIME = 4.5
RELAYED = 4.0
ACROSS = 3.0
FIRST_OWN = 3.0
FAR_READY = 11.0
PACE_DELAY = 0.0
PRODUCT_TIME = 2.7
PIECES = 2


def kernel(
    shift_ref, left_dim, right_dim, shift_any, raw_any, left, right, out,
    wave, src0, src1, src2, src3, lbuf, rbuf, acc, rs_out, rs_in, shift2, slots,
    local_sem, pair_send, pair_recv, env_local, env_send, env_recv,
    z_send, z_recv, y_send, y_recv, x_send, x_recv, rs_send, rs_recv,
):
    sources = (src0, src1, src2, src3)
    share, columns = raw_any.shape[1], raw_any.shape[2]
    terms = left.shape[0]
    m = lax.axis_index("mpo")
    s = lax.axis_index("sec")
    x, core = lax.div(m, 2), lax.rem(m, 2)
    y, z = lax.div(s, 16), lax.rem(s, 16)
    half, place = lax.div(z, 8), lax.rem(z, 8)
    other = 1 - core
    partner = 2 * x + other
    to_right, to_left = lax.rem(m + 2, 8), lax.rem(m + 6, 8)
    x_low, x_high, x_far = lax.rem(x + 3, 4), lax.rem(x + 1, 4), lax.rem(x + 2, 4)

    def along_z(step):
        return y * 16 + lax.rem(z + step + 16, 16)

    z_first = along_z(7 - 14 * core)
    y_plus = lax.rem(y + 1, 4) * 16 + z
    y_minus = lax.rem(y + 3, 4) * 16 + z
    y_next = lax.rem(y + 1 + 2 * half, 4) * 16 + z

    def rows(start, count):
        return pl.ds(pl.multiple_of(start, share), count)

    def piece(chip, side):
        return rows((2 * chip + side) * share, share)

    mine = rows(m * share, share)

    def send(src, dst, ssem, rsem, sec, mpo):
        pltpu.make_async_remote_copy(
            src_ref=src, dst_ref=dst, send_sem=ssem, recv_sem=rsem,
            device_id={"sec": sec, "mpo": mpo}, device_id_type=MESH,
        ).start()

    def await_bytes(ref, sem):
        pltpu.make_async_copy(ref, ref, sem).wait()

    load = pltpu.make_async_copy(raw_any, wave, local_sem.at[0])
    load.start()
    local = []
    local.append(pltpu.make_async_copy(left, lbuf.at[pl.ds(0, terms)], env_local.at[0]))
    local.append(pltpu.make_async_copy(right, rbuf.at[pl.ds(0, terms)], env_local.at[1]))

    barrier = pltpu.get_barrier_semaphore()

    def greet(sec, mpo):
        pl.semaphore_signal(
            barrier, inc=1, device_id={"sec": sec, "mpo": mpo}, device_id_type=MESH
        )

    for step in (7, -7):
        for core_id in range(2):
            greet(along_z(step), 2 * x + core_id)
    for sec in (along_z(2), along_z(-2), y_plus, y_minus):
        greet(sec, m)
    for k in range(1, 8):
        greet(s, lax.rem(m + k, 8))
    for copy in local:
        copy.start()
    for i in range(CHUNKS):
        sources[i][NOTHING] = jnp.zeros(sources[i].shape[1:], sources[i].dtype)
    acc[...] = jnp.zeros_like(acc)

    low_ok = place <= 6
    high_ok = place >= 1
    far_ok = jnp.where(half == 1, y <= 2, y >= 1)
    low_slot = jnp.where(low_ok, LOW, NOTHING)
    high_slot = jnp.where(high_ok, HIGH, NOTHING)
    far_low_slot = jnp.where(low_ok & far_ok, FAR_LOW, NOTHING)
    far_high_slot = jnp.where(high_ok & far_ok, FAR_HIGH, NOTHING)
    class_slots = (
        OWN,
        jnp.where(half == 1, high_slot, far_high_slot),
        jnp.where(half == 1, far_low_slot, low_slot),
        jnp.where(half == 1, low_slot, far_low_slot),
        jnp.where(half == 1, far_high_slot, high_slot),
    )

    def slot_of(shift):
        found = jnp.int32(OWN)
        for c in range(1, 5):
            found = jnp.where(shift == c, class_slots[c], found)
        return found

    row_ids = m * share + lax.broadcasted_iota(jnp.int32, (share, columns), 0)
    column_ids = lax.broadcasted_iota(jnp.int32, (share, columns), 1)
    keep = (row_ids < left_dim[0]) & (column_ids < right_dim[0])
    load.wait()
    for v in range(2 * CHUNKS):
        wave[v] = jnp.where(keep, wave[v], jnp.zeros_like(wave[v]))
    for i in range(CHUNKS):
        sources[i][OWN, mine] = wave[core * CHUNKS + i]
    pl.semaphore_wait(barrier, 15)

    def z_start(i):
        @pl.when(core == 0)
        def _():
            for core_id in range(2):
                send(
                    wave.at[core_id * CHUNKS + i], sources[i].at[LOW, mine],
                    z_send.at[i], z_recv.at[0, 0, i], along_z(7), 2 * x + core_id,
                )

        @pl.when(core == 1)
        def _():
            for core_id in range(2):
                send(
                    wave.at[core_id * CHUNKS + i], sources[i].at[HIGH, mine],
                    z_send.at[i], z_recv.at[1, 1, i], along_z(-7), 2 * x + core_id,
                )

    for i in range(PACE):
        z_start(i)
    for i in range(CHUNKS):
        send(
            wave.at[other * CHUNKS + i], sources[i].at[OWN, mine],
            pair_send.at[i], pair_recv.at[i], s, partner,
        )
    send(shift_any, shift2, env_send.at[2], env_recv.at[2], s, partner)
    send(left, lbuf.at[pl.ds(terms, terms)], env_send.at[0], env_recv.at[0], s, partner)
    send(right, rbuf.at[pl.ds(terms, terms)], env_send.at[1], env_recv.at[1], s, partner)

    def x_part(slot, i, part, to, role):
        send(part, part, x_send.at[slot, i], x_recv.at[role, slot, i], s, to)

    def y_part(slot, i, which):
        send(
            sources[i].at[slot, which], sources[i].at[slot + 2, which],
            y_send.at[slot - LOW, i], y_recv.at[slot - LOW, 0, i], y_next, m,
        )

    def x_start(slot, i, side):
        part = sources[i].at[slot, piece(x, side)]
        x_part(slot, i, part, to_right, FROM_LOW if side == 0 else REST)
        x_part(slot, i, part, to_left, FROM_HIGH if side == 1 else REST)

    def x_relay(slot, i):
        for side, chip, to in ((0, x_low, to_right), (1, x_high, to_left)):
            part = sources[i].at[slot, piece(chip, side)]
            await_bytes(part, x_recv.at[side, slot, i])
            x_part(slot, i, part, to, REST)
            if (slot, i) in GATHER_FIRST:
                y_part(slot, i, piece(chip, side))

    def x_finish(slot, i):
        await_bytes(sources[i].at[slot, pl.ds(0, 4 * share)], x_recv.at[REST, slot, i])
        if (slot, i) in GATHER_FIRST:
            y_part(slot, i, piece(x_low, 1))
            y_part(slot, i, piece(x_high, 0))
            y_part(slot, i, rows(2 * x_far * share, 2 * share))

    def own_start(i):
        await_bytes(sources[i].at[OWN, mine], pair_recv.at[i])
        x_start(OWN, i, 0)
        x_start(OWN, i, 1)

    def near_start(slot, side, i):
        await_bytes(sources[i].at[slot, piece(x, side)], z_recv.at[slot - LOW, side, i])
        which = piece(x, side)
        if slot - LOW == side:
            send(
                sources[i].at[slot, which], sources[i].at[LOW + HIGH - slot, which],
                z_send.at[i], z_recv.at[1 - side, side, i],
                along_z(2 - 4 * side), m,
            )
        if (slot, i) in GATHER_FIRST:
            y_part(slot, i, which)
        else:
            send(
                sources[i].at[slot, which], sources[i].at[slot + 2, which],
                y_send.at[slot - LOW, i], y_recv.at[slot - LOW, side, i], y_next, m,
            )
        x_start(slot, i, side)

    def far_start(slot, side, i):
        await_bytes(
            sources[i].at[slot + 2, piece(x, side)], y_recv.at[slot - LOW, side, i]
        )
        x_start(slot + 2, i, side)

    def far_finish(slot, i):
        await_bytes(sources[i].at[slot + 2], y_recv.at[slot - LOW, 0, i])

    def env_ready():
        await_bytes(shift2, env_recv.at[2])
        for t in range(terms):
            slots[t] = slot_of(shift_ref[t])
            slots[terms + t] = slot_of(shift2[t])
        local[0].wait()
        local[1].wait()
        await_bytes(lbuf.at[pl.ds(terms, terms)], env_recv.at[0])
        await_bytes(rbuf.at[pl.ds(terms, terms)], env_recv.at[1])

    def product(i, first, last):
        for t in range(first, last):
            applied = jnp.dot(
                lbuf[t], sources[i][slots[t]], preferred_element_type=jnp.float32
            ).astype(jnp.bfloat16)
            acc[...] += lax.dot_general(
                applied, rbuf[t], (((1,), (1,)), ((), ())),
                preferred_element_type=jnp.float32,
            )

    def sums_start(i):
        for k in range(8):
            rs_out[i, k] = acc[pl.ds(k * share, share), :].astype(jnp.bfloat16)
        rs_in[x, core * CHUNKS + i] = acc[mine, :].astype(jnp.bfloat16)
        for k in (4, 5, 3, 2, 6, 7, 1):
            target = lax.rem(m + k, 8)
            send(
                rs_out.at[i, target], rs_in.at[x, core * CHUNKS + i],
                rs_send.at[i], rs_recv.at[i], s, target,
            )
        acc[...] = jnp.zeros_like(acc)

    def sums_finish(i):
        await_bytes(rs_out.at[i, pl.ds(0, 7)], rs_recv.at[i])
        for v in (i, CHUNKS + i):
            total = rs_in[0, v].astype(jnp.float32)
            for k in range(1, 4):
                total = total + rs_in[k, v].astype(jnp.float32)
            out[v] = jnp.where(keep, total, jnp.zeros_like(total)).astype(out.dtype)

    plan = []

    def at(when, function, *operands):
        plan.append((when, len(plan), function, operands))

    done = 0.0
    for i in range(CHUNKS):
        at(0.1 * i, own_start, i)
        at(FIRST_OWN + 2.1 * i, x_relay, OWN, i)
        base = FIRST_NEAR + CHUNK_TIME * i
        rel = base + RELAYED
        at(base, near_start, LOW, 0, i)
        at(base, near_start, HIGH, 1, i)
        if i + PACE < CHUNKS:
            at(base + PACE_DELAY, z_start, i + PACE)
        at(rel, near_start, LOW, 1, i)
        at(rel, near_start, HIGH, 0, i)
        ready = rel + 8
        for slot in (LOW, HIGH):
            at(rel + 3, x_relay, slot, i)
            if (slot, i) in GATHER_FIRST:
                at(rel + 6, x_finish, slot, i)
                ready = max(ready, rel + FAR_READY)
            else:
                first = 0 if slot == LOW else 1
                at(base + ACROSS, far_start, slot, first, i)
                at(rel + ACROSS, far_start, slot, 1 - first, i)
                at(rel + ACROSS + 4, x_relay, slot + 2, i)
                ready = max(ready, rel + ACROSS + 8)
        done = max(done + PRODUCT_TIME, ready)
        at(done, x_finish, OWN, i)
        for slot in (LOW, HIGH):
            if (slot, i) in GATHER_FIRST:
                at(done, far_finish, slot, i)
            else:
                at(done, x_finish, slot, i)
                at(done, x_finish, slot + 2, i)
        if i == 0:
            at(done, env_ready)
        for k in range(PIECES):
            at(
                done + PRODUCT_TIME * k / PIECES, product, i,
                2 * terms * k // PIECES, 2 * terms * (k + 1) // PIECES,
            )
        at(done + PRODUCT_TIME - 0.1, sums_start, i)
        at(done + 100.0, sums_finish, i)
    for _, _, function, operands in sorted(plan, key=lambda entry: entry[:2]):
        function(*operands)

    for i in range(CHUNKS):
        await_bytes(sources[i].at[OWN, pl.ds(0, share)], pair_send.at[i])
        await_bytes(sources[i].at[OWN, pl.ds(0, 4 * share)], z_send.at[i])
        await_bytes(rs_out.at[i, pl.ds(0, 7)], rs_send.at[i])
        await_bytes(sources[i].at[OWN, pl.ds(0, 6 * share)], x_send.at[OWN, i])
        for slot in (LOW, HIGH):
            await_bytes(sources[i].at[slot, pl.ds(0, 6 * share)], x_send.at[slot, i])
            if (slot, i) in GATHER_FIRST:
                await_bytes(sources[i].at[slot], y_send.at[slot - LOW, i])
            else:
                await_bytes(
                    sources[i].at[slot, pl.ds(0, 2 * share)], y_send.at[slot - LOW, i]
                )
                await_bytes(
                    sources[i].at[slot, pl.ds(0, 6 * share)], x_send.at[slot + 2, i]
                )
    await_bytes(lbuf.at[pl.ds(0, terms)], env_send.at[0])
    await_bytes(rbuf.at[pl.ds(0, terms)], env_send.at[1])
    await_bytes(shift2, env_send.at[2])


def per_device(wavefunction, left_env, right_env, left_dims, right_dims, term_shift):
    _, vectors, share, columns = wavefunction.shape
    full = left_env.shape[2]
    terms = left_env.shape[1]
    smem = pl.BlockSpec(memory_space=pltpu.SMEM)
    anywhere = pl.BlockSpec(memory_space=pl.ANY)
    bf16 = jnp.bfloat16
    dma = pltpu.SemaphoreType.DMA
    out = pl.pallas_call(
        kernel,
        out_shape=jax.ShapeDtypeStruct((vectors, share, columns), bf16),
        in_specs=[smem, smem, smem, anywhere, anywhere, anywhere, anywhere],
        out_specs=pl.BlockSpec(memory_space=pltpu.VMEM),
        scratch_shapes=[pltpu.VMEM((vectors, share, columns), bf16)]
        + [pltpu.VMEM((6, full, columns), bf16) for _ in range(CHUNKS)]
        + [
            pltpu.VMEM((2 * terms, full, full), bf16),
            pltpu.VMEM((2 * terms, columns, columns), bf16),
            pltpu.VMEM((full, columns), jnp.float32),
            pltpu.VMEM((CHUNKS, 8, share, columns), bf16),
            pltpu.VMEM((4, vectors, share, columns), bf16),
            pltpu.SMEM((terms,), jnp.int32),
            pltpu.SMEM((2 * terms,), jnp.int32),
            dma((1,)), dma((CHUNKS,)), dma((CHUNKS,)),
            dma((2,)), dma((3,)), dma((3,)),
            dma((CHUNKS,)), dma((2, 2, CHUNKS)), dma((2, CHUNKS)), dma((2, 2, CHUNKS)),
            dma((5, CHUNKS)), dma((3, 5, CHUNKS)),
            dma((CHUNKS,)), dma((CHUNKS,)),
        ],
        compiler_params=pltpu.CompilerParams(
            collective_id=0, has_side_effects=True, vmem_limit_bytes=60 * 1024 * 1024
        ),
    )(term_shift, left_dims, right_dims, term_shift, wavefunction[0], left_env[0], right_env[0])
    return out[None]


def solution(mesh):
    in_specs = (
        P("sec", None, "mpo", None),
        P("sec", "mpo", None, None),
        P("sec", "mpo", None, None),
        P("sec"),
        P("sec"),
        P("mpo"),
    )
    out_specs = P("sec", None, "mpo", None)
    return jax.shard_map(
        per_device, mesh=mesh, in_specs=in_specs, out_specs=out_specs, check_vma=False
    )
```

```python
import jax
import jax.numpy as jnp
from jax import lax
from jax.experimental import pallas as pl
from jax.experimental.pallas import tpu as pltpu
from jax.sharding import PartitionSpec as P

SPINS = 8
MESH = pl.DeviceIdType.MESH
CHUNKS = 4
OWN, LOW, HIGH, FAR_LOW, FAR_HIGH, NOTHING = range(6)
FROM_LOW, FROM_HIGH, REST = range(3)
GATHER_FIRST = frozenset((LOW, i) for i in range(CHUNKS))
PACE = 2
FIRST_NEAR = 9.5
CHUNK_TIME = 4.5
RELAYED = 4.0
ACROSS = 3.0
FIRST_OWN = 3.0
FAR_READY = 11.0
PACE_DELAY = 3.0
PRODUCT_TIME = 2.7
PIECES = 2


def kernel(
    shift_ref, left_dim, right_dim, shift_any, raw_any, left, right, out,
    wave, src0, src1, src2, src3, lbuf, rbuf, acc, rs_out, rs_in, shift2, slots,
    local_sem, pair_send, pair_recv, env_local, env_send, env_recv,
    z_send, z_recv, y_send, y_recv, x_send, x_recv, rs_send, rs_recv,
):
    sources = (src0, src1, src2, src3)
    share, columns = raw_any.shape[1], raw_any.shape[2]
    terms = left.shape[0]
    m = lax.axis_index("mpo")
    s = lax.axis_index("sec")
    x, core = lax.div(m, 2), lax.rem(m, 2)
    y, z = lax.div(s, 16), lax.rem(s, 16)
    half, place = lax.div(z, 8), lax.rem(z, 8)
    other = 1 - core
    partner = 2 * x + other
    to_right, to_left = lax.rem(m + 2, 8), lax.rem(m + 6, 8)
    x_low, x_high, x_far = lax.rem(x + 3, 4), lax.rem(x + 1, 4), lax.rem(x + 2, 4)

    def along_z(step):
        return y * 16 + lax.rem(z + step + 16, 16)

    z_first = along_z(7 - 14 * core)
    y_plus = lax.rem(y + 1, 4) * 16 + z
    y_minus = lax.rem(y + 3, 4) * 16 + z
    y_next = lax.rem(y + 1 + 2 * half, 4) * 16 + z

    def rows(start, count):
        return pl.ds(pl.multiple_of(start, share), count)

    def piece(chip, side):
        return rows((2 * chip + side) * share, share)

    mine = rows(m * share, share)

    def send(src, dst, ssem, rsem, sec, mpo):
        pltpu.make_async_remote_copy(
            src_ref=src, dst_ref=dst, send_sem=ssem, recv_sem=rsem,
            device_id={"sec": sec, "mpo": mpo}, device_id_type=MESH,
        ).start()

    def await_bytes(ref, sem):
        pltpu.make_async_copy(ref, ref, sem).wait()

    load = pltpu.make_async_copy(raw_any, wave, local_sem.at[0])
    load.start()
    local = []
    local.append(pltpu.make_async_copy(left, lbuf.at[pl.ds(0, terms)], env_local.at[0]))
    local.append(pltpu.make_async_copy(right, rbuf.at[pl.ds(0, terms)], env_local.at[1]))

    barrier = pltpu.get_barrier_semaphore()

    def greet(sec, mpo):
        pl.semaphore_signal(
            barrier, inc=1, device_id={"sec": sec, "mpo": mpo}, device_id_type=MESH
        )

    for step in (7, -7):
        for core_id in range(2):
            greet(along_z(step), 2 * x + core_id)
    for sec in (along_z(2), along_z(-2), y_plus, y_minus):
        greet(sec, m)
    for k in range(1, 8):
        greet(s, lax.rem(m + k, 8))
    for copy in local:
        copy.start()
    for i in range(CHUNKS):
        sources[i][NOTHING] = jnp.zeros(sources[i].shape[1:], sources[i].dtype)
    acc[...] = jnp.zeros_like(acc)

    low_ok = place <= 6
    high_ok = place >= 1
    far_ok = jnp.where(half == 1, y <= 2, y >= 1)
    low_slot = jnp.where(low_ok, LOW, NOTHING)
    high_slot = jnp.where(high_ok, HIGH, NOTHING)
    far_low_slot = jnp.where(low_ok & far_ok, FAR_LOW, NOTHING)
    far_high_slot = jnp.where(high_ok & far_ok, FAR_HIGH, NOTHING)
    class_slots = (
        OWN,
        jnp.where(half == 1, high_slot, far_high_slot),
        jnp.where(half == 1, far_low_slot, low_slot),
        jnp.where(half == 1, low_slot, far_low_slot),
        jnp.where(half == 1, far_high_slot, high_slot),
    )

    def slot_of(shift):
        found = jnp.int32(OWN)
        for c in range(1, 5):
            found = jnp.where(shift == c, class_slots[c], found)
        return found

    row_ids = m * share + lax.broadcasted_iota(jnp.int32, (share, columns), 0)
    column_ids = lax.broadcasted_iota(jnp.int32, (share, columns), 1)
    keep = (row_ids < left_dim[0]) & (column_ids < right_dim[0])
    load.wait()
    for v in range(2 * CHUNKS):
        wave[v] = jnp.where(keep, wave[v], jnp.zeros_like(wave[v]))
    for i in range(CHUNKS):
        sources[i][OWN, mine] = wave[core * CHUNKS + i]
    pl.semaphore_wait(barrier, 15)

    def z_start(i):
        @pl.when(core == 0)
        def _():
            for core_id in range(2):
                send(
                    wave.at[core_id * CHUNKS + i], sources[i].at[LOW, mine],
                    z_send.at[i], z_recv.at[0, 0, i], along_z(7), 2 * x + core_id,
                )

        @pl.when(core == 1)
        def _():
            for core_id in range(2):
                send(
                    wave.at[core_id * CHUNKS + i], sources[i].at[HIGH, mine],
                    z_send.at[i], z_recv.at[1, 1, i], along_z(-7), 2 * x + core_id,
                )

    for i in range(PACE):
        z_start(i)
    for i in range(CHUNKS):
        send(
            wave.at[other * CHUNKS + i], sources[i].at[OWN, mine],
            pair_send.at[i], pair_recv.at[i], s, partner,
        )
    send(shift_any, shift2, env_send.at[2], env_recv.at[2], s, partner)
    send(left, lbuf.at[pl.ds(terms, terms)], env_send.at[0], env_recv.at[0], s, partner)
    send(right, rbuf.at[pl.ds(terms, terms)], env_send.at[1], env_recv.at[1], s, partner)

    def x_part(slot, i, part, to, role):
        send(part, part, x_send.at[slot, i], x_recv.at[role, slot, i], s, to)

    def y_part(slot, i, which):
        send(
            sources[i].at[slot, which], sources[i].at[slot + 2, which],
            y_send.at[slot - LOW, i], y_recv.at[slot - LOW, 0, i], y_next, m,
        )

    def x_start(slot, i, side):
        part = sources[i].at[slot, piece(x, side)]
        x_part(slot, i, part, to_right, FROM_LOW if side == 0 else REST)
        x_part(slot, i, part, to_left, FROM_HIGH if side == 1 else REST)

    def x_relay(slot, i):
        for side, chip, to in ((0, x_low, to_right), (1, x_high, to_left)):
            part = sources[i].at[slot, piece(chip, side)]
            await_bytes(part, x_recv.at[side, slot, i])
            x_part(slot, i, part, to, REST)
            if (slot, i) in GATHER_FIRST:
                y_part(slot, i, piece(chip, side))

    def x_finish(slot, i):
        await_bytes(sources[i].at[slot, pl.ds(0, 4 * share)], x_recv.at[REST, slot, i])
        if (slot, i) in GATHER_FIRST:
            y_part(slot, i, piece(x_low, 1))
            y_part(slot, i, piece(x_high, 0))
            y_part(slot, i, rows(2 * x_far * share, 2 * share))

    def own_start(i):
        await_bytes(sources[i].at[OWN, mine], pair_recv.at[i])
        x_start(OWN, i, 0)
        x_start(OWN, i, 1)

    def near_start(slot, side, i):
        await_bytes(sources[i].at[slot, piece(x, side)], z_recv.at[slot - LOW, side, i])
        which = piece(x, side)
        if slot - LOW == side:
            send(
                sources[i].at[slot, which], sources[i].at[LOW + HIGH - slot, which],
                z_send.at[i], z_recv.at[1 - side, side, i],
                along_z(2 - 4 * side), m,
            )
        if (slot, i) in GATHER_FIRST:
            y_part(slot, i, which)
        else:
            send(
                sources[i].at[slot, which], sources[i].at[slot + 2, which],
                y_send.at[slot - LOW, i], y_recv.at[slot - LOW, side, i], y_next, m,
            )
        x_start(slot, i, side)

    def far_start(slot, side, i):
        await_bytes(
            sources[i].at[slot + 2, piece(x, side)], y_recv.at[slot - LOW, side, i]
        )
        x_start(slot + 2, i, side)

    def far_finish(slot, i):
        await_bytes(sources[i].at[slot + 2], y_recv.at[slot - LOW, 0, i])

    def env_ready():
        await_bytes(shift2, env_recv.at[2])
        for t in range(terms):
            slots[t] = slot_of(shift_ref[t])
            slots[terms + t] = slot_of(shift2[t])
        local[0].wait()
        local[1].wait()
        await_bytes(lbuf.at[pl.ds(terms, terms)], env_recv.at[0])
        await_bytes(rbuf.at[pl.ds(terms, terms)], env_recv.at[1])

    def product(i, first, last):
        for t in range(first, last):
            applied = jnp.dot(
                lbuf[t], sources[i][slots[t]], preferred_element_type=jnp.float32
            ).astype(jnp.bfloat16)
            acc[...] += lax.dot_general(
                applied, rbuf[t], (((1,), (1,)), ((), ())),
                preferred_element_type=jnp.float32,
            )

    def sums_start(i):
        for k in range(8):
            rs_out[i, k] = acc[pl.ds(k * share, share), :].astype(jnp.bfloat16)
        rs_in[x, core * CHUNKS + i] = acc[mine, :].astype(jnp.bfloat16)
        for k in (4, 5, 3, 2, 6, 7, 1):
            target = lax.rem(m + k, 8)
            send(
                rs_out.at[i, target], rs_in.at[x, core * CHUNKS + i],
                rs_send.at[i], rs_recv.at[i], s, target,
            )
        acc[...] = jnp.zeros_like(acc)

    def sums_finish(i):
        await_bytes(rs_out.at[i, pl.ds(0, 7)], rs_recv.at[i])
        for v in (i, CHUNKS + i):
            total = rs_in[0, v].astype(jnp.float32)
            for k in range(1, 4):
                total = total + rs_in[k, v].astype(jnp.float32)
            out[v] = jnp.where(keep, total, jnp.zeros_like(total)).astype(out.dtype)

    plan = []

    def at(when, function, *operands):
        plan.append((when, len(plan), function, operands))

    done = 0.0
    for i in range(CHUNKS):
        at(0.1 * i, own_start, i)
        at(FIRST_OWN + 2.1 * i, x_relay, OWN, i)
        base = FIRST_NEAR + CHUNK_TIME * i
        rel = base + RELAYED
        at(base, near_start, LOW, 0, i)
        at(base, near_start, HIGH, 1, i)
        if i + PACE < CHUNKS:
            at(base + PACE_DELAY, z_start, i + PACE)
        at(rel, near_start, LOW, 1, i)
        at(rel, near_start, HIGH, 0, i)
        ready = rel + 8
        for slot in (LOW, HIGH):
            at(rel + 3, x_relay, slot, i)
            if (slot, i) in GATHER_FIRST:
                at(rel + 6, x_finish, slot, i)
                ready = max(ready, rel + FAR_READY)
            else:
                first = 0 if slot == LOW else 1
                at(base + ACROSS, far_start, slot, first, i)
                at(rel + ACROSS, far_start, slot, 1 - first, i)
                at(rel + ACROSS + 4, x_relay, slot + 2, i)
                ready = max(ready, rel + ACROSS + 8)
        done = max(done + PRODUCT_TIME, ready)
        at(done, x_finish, OWN, i)
        for slot in (LOW, HIGH):
            if (slot, i) in GATHER_FIRST:
                at(done, far_finish, slot, i)
            else:
                at(done, x_finish, slot, i)
                at(done, x_finish, slot + 2, i)
        if i == 0:
            at(done, env_ready)
        for k in range(PIECES):
            at(
                done + PRODUCT_TIME * k / PIECES, product, i,
                2 * terms * k // PIECES, 2 * terms * (k + 1) // PIECES,
            )
        at(done + PRODUCT_TIME - 0.1, sums_start, i)
        at(done + 100.0, sums_finish, i)
    for _, _, function, operands in sorted(plan, key=lambda entry: entry[:2]):
        function(*operands)

    for i in range(CHUNKS):
        await_bytes(sources[i].at[OWN, pl.ds(0, share)], pair_send.at[i])
        await_bytes(sources[i].at[OWN, pl.ds(0, 4 * share)], z_send.at[i])
        await_bytes(rs_out.at[i, pl.ds(0, 7)], rs_send.at[i])
        await_bytes(sources[i].at[OWN, pl.ds(0, 6 * share)], x_send.at[OWN, i])
        for slot in (LOW, HIGH):
            await_bytes(sources[i].at[slot, pl.ds(0, 6 * share)], x_send.at[slot, i])
            if (slot, i) in GATHER_FIRST:
                await_bytes(sources[i].at[slot], y_send.at[slot - LOW, i])
            else:
                await_bytes(
                    sources[i].at[slot, pl.ds(0, 2 * share)], y_send.at[slot - LOW, i]
                )
                await_bytes(
                    sources[i].at[slot, pl.ds(0, 6 * share)], x_send.at[slot + 2, i]
                )
    await_bytes(lbuf.at[pl.ds(0, terms)], env_send.at[0])
    await_bytes(rbuf.at[pl.ds(0, terms)], env_send.at[1])
    await_bytes(shift2, env_send.at[2])


def per_device(wavefunction, left_env, right_env, left_dims, right_dims, term_shift):
    _, vectors, share, columns = wavefunction.shape
    full = left_env.shape[2]
    terms = left_env.shape[1]
    smem = pl.BlockSpec(memory_space=pltpu.SMEM)
    anywhere = pl.BlockSpec(memory_space=pl.ANY)
    bf16 = jnp.bfloat16
    dma = pltpu.SemaphoreType.DMA
    out = pl.pallas_call(
        kernel,
        out_shape=jax.ShapeDtypeStruct((vectors, share, columns), bf16),
        in_specs=[smem, smem, smem, anywhere, anywhere, anywhere, anywhere],
        out_specs=pl.BlockSpec(memory_space=pltpu.VMEM),
        scratch_shapes=[pltpu.VMEM((vectors, share, columns), bf16)]
        + [pltpu.VMEM((6, full, columns), bf16) for _ in range(CHUNKS)]
        + [
            pltpu.VMEM((2 * terms, full, full), bf16),
            pltpu.VMEM((2 * terms, columns, columns), bf16),
            pltpu.VMEM((full, columns), jnp.float32),
            pltpu.VMEM((CHUNKS, 8, share, columns), bf16),
            pltpu.VMEM((4, vectors, share, columns), bf16),
            pltpu.SMEM((terms,), jnp.int32),
            pltpu.SMEM((2 * terms,), jnp.int32),
            dma((1,)), dma((CHUNKS,)), dma((CHUNKS,)),
            dma((2,)), dma((3,)), dma((3,)),
            dma((CHUNKS,)), dma((2, 2, CHUNKS)), dma((2, CHUNKS)), dma((2, 2, CHUNKS)),
            dma((5, CHUNKS)), dma((3, 5, CHUNKS)),
            dma((CHUNKS,)), dma((CHUNKS,)),
        ],
        compiler_params=pltpu.CompilerParams(
            collective_id=0, has_side_effects=True, vmem_limit_bytes=60 * 1024 * 1024
        ),
    )(term_shift, left_dims, right_dims, term_shift, wavefunction[0], left_env[0], right_env[0])
    return out[None]


def solution(mesh):
    in_specs = (
        P("sec", None, "mpo", None),
        P("sec", "mpo", None, None),
        P("sec", "mpo", None, None),
        P("sec"),
        P("sec"),
        P("mpo"),
    )
    out_specs = P("sec", None, "mpo", None)
    return jax.shard_map(
        per_device, mesh=mesh, in_specs=in_specs, out_specs=out_specs, check_vma=False
    )
```
